32 devices in a mesh: clip: 4 (over y, core), frame: 8 (over z, x).
Axes of the slice: x: 2, y: 2, z: 4, core: 2. Of those that a mesh axis runs over, the one named last changes fastest.
Arguments:
- video: bfloat16 [128, 512, 512], P(('clip', 'frame')), parts along dimension 0, may hold values from -6 to 6
- timestep: int32 [4], P('clip'), parts along dimension 0, may hold values from 0 to 999
- cond_weight: bfloat16 [128, 2048], replicated, may hold values from -0.5 to 0.5
- spatial_gain: float32 [512], replicated, may hold values from 0.25 to 1.75
- spatial_qkv: bfloat16 [512, 1536], replicated, may hold values from -0.25 to 0.25
- spatial_out: bfloat16 [512, 512], replicated, may hold values from -0.25 to 0.25
- temporal_gain: float32 [512], replicated, may hold values from 0.25 to 1.75
- temporal_qkv: bfloat16 [512, 1536], replicated, may hold values from -0.25 to 0.25
- temporal_out: bfloat16 [512, 512], replicated, may hold values from -0.25 to 0.25
- merge_weight: bfloat16 [4096, 1024], replicated, may hold values from -0.09375 to 0.09375
- coarse_gain: float32 [1024], replicated, may hold values from 0.25 to 1.75
- coarse_qkv: bfloat16 [1024, 3072], replicated, may hold values from -0.1875 to 0.1875
- coarse_out: bfloat16 [1024, 1024], replicated, may hold values from -0.1875 to 0.1875
- up_weight: bfloat16 [1024, 512], replicated, may hold values from -0.1875 to 0.1875
Outputs:
- denoised: bfloat16 [128, 512, 512], P(('clip', 'frame')), parts along dimension 0
The draws below stay inside these ranges and needn't reach their ends.
There are 4 independent parts, one for each index of `clip`. The reference program is written for one: setup_inputs(seed, part) draws one part's arguments, and reference() takes and returns one part's arrays. A program takes and returns all parts, laid end to end along the dimension named above; an argument that names none is the same for every part. Nothing has to cross between parts.
All inputs are finite; a program needn't handle non-finite values.
Results may differ from the reference program's by a relative error of at most 0.015.
Values may be sent and summed in bfloat16 or wider, within the bound.
No kernel may reach another device: no remote copies, remote signals or barrier semaphores. Data moves between devices by JAX's collectives and lax.ppermute only.
A program may use at most 192 MiB of HBM per device.

```python
import math
import jax
import jax.numpy as jnp
from jax import lax

D = 512
DC = 1024
HEAD = 64
FREQ = 64
TOK = 512
FRAMES = 32
BLK = 128


def levels(own_key, extent, cuts, low, largest):
    def one(dim, parts):
        draws = jax.random.uniform(jax.random.fold_in(jax.random.fold_in(own_key, 6), dim), (parts,), jnp.float32, low / len(cuts), largest / len(cuts))
        return jnp.repeat(jnp.exp(draws), extent[dim] // parts).reshape((-1,) + (1,) * (len(extent) - dim - 1))

    factor_of = one(*cuts[0])
    for cut in cuts[1:]:
        factor_of = factor_of * one(*cut)
    return factor_of


def centred(stream_key, extent, width, limit, shards=(), kind=jnp.bfloat16):
    factor_of = levels(stream_key, extent, shards, -0.22, 0.18) if shards else 1.0
    array = jax.random.normal(stream_key, extent, jnp.float32) * width * factor_of
    return jnp.minimum(jnp.maximum(array, -limit), limit).astype(kind)


def setup_inputs(seed: int = 0, part: int = 0) -> dict:
    seeds = jax.random.split(jax.random.key(seed), 15)
    part_splits = jax.random.split(jax.random.fold_in(seeds[14], part), 15)
    return {
        "video": centred(part_splits[0], (FRAMES, TOK, D), 1.0, 6.0, ((0, 8),)),
        "timestep": jax.random.randint(part_splits[1], (1,), 0, 1000).astype(jnp.int32),
        "cond_weight": centred(seeds[2], (2 * FREQ, 4 * D), (2 * FREQ) ** -0.5, 0.5),
        "spatial_gain": jnp.clip(1.0 + 0.15 * jax.random.normal(seeds[3], (D,), jnp.float32), 0.25, 1.75),
        "spatial_qkv": centred(seeds[4], (D, 3 * D), D ** -0.5, 0.25),
        "spatial_out": centred(seeds[5], (D, D), D ** -0.5, 0.25),
        "temporal_gain": jnp.clip(1.0 + 0.15 * jax.random.normal(seeds[6], (D,), jnp.float32), 0.25, 1.75),
        "temporal_qkv": centred(seeds[7], (D, 3 * D), D ** -0.5, 0.25),
        "temporal_out": centred(seeds[8], (D, D), D ** -0.5, 0.25),
        "merge_weight": centred(seeds[9], (8 * D, DC), (8 * D) ** -0.5, 0.09375),
        "coarse_gain": jnp.clip(1.0 + 0.15 * jax.random.normal(seeds[10], (DC,), jnp.float32), 0.25, 1.75),
        "coarse_qkv": centred(seeds[11], (DC, 3 * DC), DC ** -0.5, 0.1875),
        "coarse_out": centred(seeds[12], (DC, DC), DC ** -0.5, 0.1875),
        "up_weight": centred(seeds[13], (DC, D), DC ** -0.5, 0.1875),
    }


def modulation_of(timestep, cond_weight):
    counter = jnp.arange(FREQ, dtype=jnp.float32)
    frequency = jnp.exp(counter * (-math.log(10000.0) / FREQ))
    angles = timestep.astype(jnp.float32)[0] * frequency
    embedding = jnp.concatenate([jnp.sin(angles), jnp.cos(angles)])
    return jnp.dot(embedding[None, :], cond_weight.astype(jnp.float32), precision=lax.Precision.HIGHEST)[0]

def attention_block(inputs, gain_vec, scale_mod, shift_mod, w_qkv, w_out, head_count):
    length, batched, features = inputs.shape
    widened = inputs.astype(jnp.float32)
    mean_square = lax.optimization_barrier(jnp.mean(widened * widened, axis=-1, keepdims=True))
    normed = (widened * lax.rsqrt(mean_square + 1e-06) * gain_vec * (1.0 + scale_mod) + shift_mod).astype(jnp.bfloat16)
    projected = jnp.dot(normed.reshape(length * batched, features), w_qkv, preferred_element_type=jnp.float32)
    projected = projected.astype(jnp.bfloat16).reshape(length, batched, 3, head_count, features // head_count)
    queries = projected[:, :, 0].astype(jnp.float32)
    keys = projected[:, :, 1].astype(jnp.float32)
    values = projected[:, :, 2].astype(jnp.float32)
    scores = jnp.einsum('snhe,tnhe->nhst', queries, keys) * (1.0 / math.sqrt(features // head_count))
    probs = jax.nn.softmax(scores, axis=-1).astype(jnp.bfloat16)
    mixed = jnp.einsum('nhst,tnhe->snhe', probs.astype(jnp.float32), values)
    mixed = mixed.astype(jnp.bfloat16).reshape(length * batched, features)
    update = jnp.dot(mixed, w_out, preferred_element_type=jnp.float32).reshape(length, batched, features)
    return (widened + update).astype(jnp.bfloat16)

def merge_frames(fine_tokens, merge_weight):
    frames_here, blocks, quads, features = fine_tokens.shape
    paired = fine_tokens.reshape(frames_here // 2, 2, blocks, quads, features).transpose(0, 2, 1, 3, 4)
    paired = paired.reshape(frames_here // 2 * blocks, 2 * quads * features)
    merged = jnp.dot(paired, merge_weight, preferred_element_type=jnp.float32).astype(jnp.bfloat16)
    return merged.reshape(frames_here // 2, blocks, merge_weight.shape[1])

def combine_levels(fine_tokens, coarse_tokens, up_weight):
    frames_here, blocks, quads, features = fine_tokens.shape
    upsampled = jnp.dot(coarse_tokens.reshape(-1, coarse_tokens.shape[2]), up_weight, preferred_element_type=jnp.float32)
    upsampled = upsampled.reshape(frames_here // 2, 1, blocks, 1, features)
    result = fine_tokens.astype(jnp.float32).reshape(frames_here // 2, 2, blocks, quads, features) + upsampled
    return result.astype(jnp.bfloat16).reshape(fine_tokens.shape)

def reference(video, timestep, cond_weight, spatial_gain, spatial_qkv, spatial_out, temporal_gain, temporal_qkv, temporal_out, merge_weight, coarse_gain, coarse_qkv, coarse_out, up_weight):
    modulation = modulation_of(timestep, cond_weight)
    scale_s, shift_s, scale_t, shift_t = [modulation[i * D:(i + 1) * D] for i in range(4)]

    def spatial(frame_rows):
        return attention_block(frame_rows[:, None, :], spatial_gain, scale_s, shift_s, spatial_qkv, spatial_out, D // HEAD)[:, 0, :]
    fine1 = lax.map(spatial, video)
    grouped = jnp.moveaxis(fine1.reshape(FRAMES, BLK, 4, D), 1, 0)

    def temporal(cell_rows):
        return attention_block(cell_rows, temporal_gain, scale_t, shift_t, temporal_qkv, temporal_out, D // HEAD)
    fine2 = jnp.moveaxis(lax.map(temporal, grouped), 0, 1)
    coarse0 = merge_frames(fine2, merge_weight)
    coarse1 = attention_block(coarse0, coarse_gain, 0.0, 0.0, coarse_qkv, coarse_out, DC // HEAD)
    return combine_levels(fine2, coarse1, up_weight).reshape(FRAMES, TOK, D)
```

```python
import math

import jax
import jax.numpy as jnp
from jax import lax
from jax.experimental import pallas as pl
from jax.experimental.pallas import tpu as pltpu
from jax.sharding import PartitionSpec as P

D = 512
DC = 1024
HEAD = 64
FREQ = 64


def modulation_of(timestep, cond_weight):
    counter = jnp.arange(FREQ, dtype=jnp.float32)
    frequency = jnp.exp(counter * (-math.log(10000.0) / FREQ))
    angles = timestep.astype(jnp.float32)[0] * frequency
    embedding = jnp.concatenate([jnp.sin(angles), jnp.cos(angles)])
    return jnp.dot(
        embedding[None, :], cond_weight.astype(jnp.float32), precision=lax.Precision.HIGHEST
    )[0]


def attention_block(inputs, gain_vec, scale_mod, shift_mod, w_qkv, w_out, head_count):
    length, batched, features = inputs.shape
    widened = inputs.astype(jnp.float32)
    mean_square = jnp.mean(widened * widened, axis=-1, keepdims=True)
    normed = (
        widened * lax.rsqrt(mean_square + 1e-06) * gain_vec * (1.0 + scale_mod) + shift_mod
    ).astype(jnp.bfloat16)
    projected = jnp.dot(
        normed.reshape(length * batched, features), w_qkv, preferred_element_type=jnp.float32
    )
    projected = projected.astype(jnp.bfloat16).reshape(
        length, batched, 3, head_count, features // head_count
    )
    queries = projected[:, :, 0]
    keys = projected[:, :, 1]
    values = projected[:, :, 2]
    scores = jnp.einsum("snhe,tnhe->nhst", queries, keys, preferred_element_type=jnp.float32) * (
        1.0 / math.sqrt(features // head_count)
    )
    probs = jax.nn.softmax(scores, axis=-1).astype(jnp.bfloat16)
    mixed = jnp.einsum("nhst,tnhe->snhe", probs, values, preferred_element_type=jnp.float32)
    mixed = mixed.astype(jnp.bfloat16).reshape(length * batched, features)
    update = jnp.dot(mixed, w_out, preferred_element_type=jnp.float32).reshape(
        length, batched, features
    )
    return (widened + update).astype(jnp.bfloat16)


def merge_frames(fine_tokens, merge_weight):
    frames_here, blocks, quads, features = fine_tokens.shape
    paired = fine_tokens.reshape(frames_here // 2, 2, blocks, quads, features).transpose(
        0, 2, 1, 3, 4
    )
    paired = paired.reshape(frames_here // 2 * blocks, 2 * quads * features)
    merged = jnp.dot(paired, merge_weight, preferred_element_type=jnp.float32).astype(jnp.bfloat16)
    return merged.reshape(frames_here // 2, blocks, merge_weight.shape[1])


def combine_levels(fine_tokens, coarse_tokens, up_weight):
    frames_here, blocks, quads, features = fine_tokens.shape
    upsampled = jnp.dot(
        coarse_tokens.reshape(-1, coarse_tokens.shape[2]),
        up_weight,
        preferred_element_type=jnp.float32,
    )
    upsampled = upsampled.reshape(frames_here // 2, 1, blocks, 1, features)
    result = (
        fine_tokens.astype(jnp.float32).reshape(frames_here // 2, 2, blocks, quads, features)
        + upsampled
    )
    return result.astype(jnp.bfloat16).reshape(fine_tokens.shape)


def body_small(
    video,
    timestep,
    cond_weight,
    spatial_gain,
    spatial_qkv,
    spatial_out,
    temporal_gain,
    temporal_qkv,
    temporal_out,
    merge_weight,
    coarse_gain,
    coarse_qkv,
    coarse_out,
    up_weight,
):
    frames_local, tokens_frame, features = video.shape
    groups = lax.axis_size("frame")
    cells_local = tokens_frame // 4 // groups
    modulation = modulation_of(timestep, cond_weight)
    scale_s, shift_s, scale_t, shift_t = [modulation[i * D : (i + 1) * D] for i in range(4)]

    def spatial(frame_rows):
        return attention_block(
            frame_rows[:, None, :],
            spatial_gain,
            scale_s,
            shift_s,
            spatial_qkv,
            spatial_out,
            D // HEAD,
        )[:, 0, :]

    fine1 = lax.map(spatial, video)
    grouped = fine1.reshape(frames_local, groups, cells_local, 4, features)
    cell_view = lax.all_to_all(grouped, "frame", split_axis=1, concat_axis=0, tiled=True)
    length = cell_view.shape[0]
    single = cell_view.shape[1]
    blocks = cell_view.shape[2]
    cell_rows = cell_view.reshape(length, single * blocks, 4, features)
    temporal_length = cell_rows.shape[0]
    temporal_blocks = cell_rows.shape[1]
    mixed = attention_block(
        cell_rows.reshape(temporal_length, temporal_blocks * 4, features),
        temporal_gain,
        scale_t,
        shift_t,
        temporal_qkv,
        temporal_out,
        D // HEAD,
    )
    fine2 = mixed.reshape(cell_rows.shape)
    coarse0 = merge_frames(fine2, merge_weight)
    coarse1 = attention_block(coarse0, coarse_gain, 0.0, 0.0, coarse_qkv, coarse_out, DC // HEAD)
    exchanged = combine_levels(fine2, coarse1, up_weight).reshape(cell_view.shape)
    result = lax.all_to_all(exchanged, "frame", split_axis=0, concat_axis=1, tiled=True)
    return result.reshape(frames_local, tokens_frame, features)


CHUNKS = 2
LOG2E = math.log2(math.e)
ANY = pl.BlockSpec(memory_space=pl.ANY)
VMEM = pl.BlockSpec(memory_space=pltpu.VMEM)


def dot(a, b):
    return jnp.dot(a, b, preferred_element_type=jnp.float32)


def dot_t(a, b):
    return lax.dot_general(a, b, (((1,), (1,)), ((), ())), preferred_element_type=jnp.float32)


def normed_rows(x, gain, shift):
    mean_square = jnp.mean(x * x, axis=-1, keepdims=True)
    y = x * lax.rsqrt(mean_square + 1e-06) * gain
    return (y if shift is None else y + shift).astype(jnp.bfloat16)


def project(normed, w_ref, qkv_ref, width, step=512):
    for i in range(0, 3 * width, step):
        part = dot(normed, w_ref[:, i : i + step])
        if i < width:
            part = part * (LOG2E / math.sqrt(HEAD))
        qkv_ref[:, i : i + step] = part.astype(jnp.bfloat16)


def attend(qkv_ref, mixed_ref, width, bias, block):
    rows = qkv_ref.shape[0]
    low = lax.broadcasted_iota(jnp.int32, (1, 2 * HEAD), 1) < HEAD
    for pair in range(width // (2 * HEAD)):
        at = pair * 2 * HEAD
        keys = qkv_ref[:, width + at : width + at + 2 * HEAD]
        values = qkv_ref[:, 2 * width + at : 2 * width + at + 2 * HEAD]
        zero = jnp.zeros_like(keys)
        one = jnp.ones_like(keys)
        sides = (
            (jnp.where(low, keys, zero), jnp.where(low, values, one)),
            (jnp.where(low, zero, keys), jnp.where(low, one, values)),
        )
        for r in range(0, rows, block):
            queries = qkv_ref[r : r + block, at : at + 2 * HEAD]
            got = []
            for k_side, v_side in sides:
                scores = dot_t(queries, k_side)
                if bias is not None:
                    scores = scores + bias
                probs = jnp.exp2(scores - jnp.max(scores, axis=-1, keepdims=True))
                got.append(dot(probs.astype(jnp.bfloat16), v_side))
            top = jnp.where(low, got[0], got[1])
            sums = pltpu.roll(jnp.where(low, got[1], got[0]), HEAD, 1)
            mixed_ref[r : r + block, at : at + 2 * HEAD] = (top / sums).astype(jnp.bfloat16)


def spatial_kernel(
    n, x_ref, gain_ref, shift_ref, w_ref, wo_ref, *rest
):
    outs, (xs, xp, qkv, mixed) = rest[:-4], rest[-4:]
    tokens, width = mixed.shape
    cells = tokens // 4
    part = cells // n // CHUNKS
    for j in range(width // 128):
        xs[j] = x_ref[0, :, j * 128 : (j + 1) * 128].astype(jnp.float32)
        for q in range(4):
            xp[q, :, j * 128 : (j + 1) * 128] = xs[j, pl.ds(q, cells, stride=4), :]
    x = xp[...].reshape(tokens, width)
    project(normed_rows(x, gain_ref[...], shift_ref[...]), w_ref, qkv, width)
    attend(qkv, mixed, width, None, 256)
    done = xp[...].reshape(tokens, width) + dot(mixed[...], wo_ref[...])
    xp[...] = done.reshape(xp.shape)
    for s in range(n):
        for c in range(CHUNKS):
            first = (s * CHUNKS + c) * part
            outs[c][s] = xp[:, first : first + part, :].astype(jnp.bfloat16)


def spatial_call(n, frame, video, gain, shift, w, wo):
    _, tokens, width = video.shape
    part = tokens // 4 // n // CHUNKS
    return pl.pallas_call(
        lambda *refs: spatial_kernel(n, *refs),
        grid=(1,),
        in_specs=[
            pl.BlockSpec((1, tokens, width), lambda i: (frame, 0, 0)),
            VMEM,
            VMEM,
            VMEM,
            VMEM,
        ],
        out_specs=[VMEM] * CHUNKS,
        out_shape=[jax.ShapeDtypeStruct((n, 4, part, width), jnp.bfloat16)] * CHUNKS,
        scratch_shapes=[
            pltpu.VMEM((width // 128, tokens, 128), jnp.float32),
            pltpu.VMEM((4, tokens // 4, width), jnp.float32),
            pltpu.VMEM((tokens, 3 * width), jnp.bfloat16),
            pltpu.VMEM((tokens, width), jnp.bfloat16),
        ],
        cost_estimate=pl.CostEstimate(
            flops=8 * tokens * width * width + 8 * tokens * tokens * width,
            bytes_accessed=8 * width * width + 4 * tokens * width,
            transcendentals=tokens * tokens * width // HEAD,
        ),
        name="spatial",
    )(video, gain, shift, w, wo)


def same_cell(rows, part):
    a = lax.rem(lax.broadcasted_iota(jnp.int32, (rows, rows), 0), part)
    b = lax.rem(lax.broadcasted_iota(jnp.int32, (rows, rows), 1), part)
    return jnp.where(a == b, 0.0, -1e30).astype(jnp.float32)


def window_kernel(n, frames, part, *refs):
    pieces, refs = refs[:frames], refs[frames:]
    gain, shift, coarse_gain, *hbm, out_ref = refs[:10]
    xs, qkv, mixed, bias, cqkv, cmixed, *held, sems = refs[10:]
    copies = [pltpu.make_async_copy(hbm[i], held[i], sems.at[i]) for i in range(6)]
    for copy in copies:
        copy.start()
    wt, wto, wm, wc, wco, wu = held
    rows, width = mixed.shape
    coarse_rows, coarse_width = cmixed.shape
    bias[...] = same_cell(rows, part)
    for s in range(n):
        for f in range(frames):
            at = (s * frames + f) * part
            for q in range(4):
                xs[q, at : at + part, :] = pieces[f][s, q].astype(jnp.float32)
    copies[0].wait()
    copies[1].wait()

    def temporal(q, carry):
        project(normed_rows(xs[q], gain[...], shift[...]), wt, qkv, width)
        attend(qkv, mixed, width, bias[...], rows)
        fine = xs[q] + dot(mixed[...], wto[...])
        xs[q] = fine.astype(jnp.bfloat16).astype(jnp.float32)
        return carry

    lax.fori_loop(0, 4, temporal, 0)
    copies[2].wait()
    coarse = None
    for d in range(2):
        for q in range(4):
            fine = xs[q].reshape(coarse_rows // part, 2, part, width)[:, d]
            fine = fine.reshape(coarse_rows, width).astype(jnp.bfloat16)
            at = (d * 4 + q) * width
            term = dot(fine, wm[at : at + width, :])
            coarse = term if coarse is None else coarse + term
    coarse = coarse.astype(jnp.bfloat16).astype(jnp.float32)
    copies[3].wait()
    project(normed_rows(coarse, coarse_gain[...], None), wc, cqkv, coarse_width)
    attend(cqkv, cmixed, coarse_width, bias[:coarse_rows, :coarse_rows], coarse_rows)
    copies[4].wait()
    coarse = (coarse + dot(cmixed[...], wco[...])).astype(jnp.bfloat16)
    copies[5].wait()
    up = dot(coarse, wu[...])
    for s in range(n):
        for f in range(frames):
            at = (s * frames + f) * part
            pair = at // (2 * part) * part
            for q in range(4):
                done = xs[q, at : at + part, :] + up[pair : pair + part]
                out_ref[s, f, q] = done.astype(jnp.bfloat16)


def window_call(n, frames, pieces, vectors, weights):
    part, width = pieces[0].shape[2:]
    rows = n * frames * part
    coarse_width = weights[3].shape[0]
    flops = 2 * 4 * rows * (4 * width * width) + rows * 8 * width * coarse_width
    flops += rows * (4 * coarse_width * coarse_width + coarse_width * width)
    return pl.pallas_call(
        lambda *refs: window_kernel(n, frames, part, *refs),
        in_specs=[VMEM] * (frames + 3) + [ANY] * 6,
        out_specs=VMEM,
        out_shape=jax.ShapeDtypeStruct((n, frames, 4, part, width), jnp.bfloat16),
        scratch_shapes=[
            pltpu.VMEM((4, rows, width), jnp.float32),
            pltpu.VMEM((rows, 3 * width), jnp.bfloat16),
            pltpu.VMEM((rows, width), jnp.bfloat16),
            pltpu.VMEM((rows, rows), jnp.float32),
            pltpu.VMEM((rows // 2, 3 * coarse_width), jnp.bfloat16),
            pltpu.VMEM((rows // 2, coarse_width), jnp.bfloat16),
        ]
        + [pltpu.VMEM(w.shape, w.dtype) for w in weights]
        + [pltpu.SemaphoreType.DMA((6,))],
        cost_estimate=pl.CostEstimate(
            flops=flops,
            bytes_accessed=sum(w.size for w in weights) * 2 + 16 * rows * width,
            transcendentals=4 * rows * rows * width // HEAD,
        ),
        name="window",
    )(*pieces, *vectors, *weights)


def assemble_kernel(n, part, *refs):
    pieces, out_ref, scratch = refs[:-2], refs[-2], refs[-1]
    for s in range(n):
        for c in range(CHUNKS):
            first = (s * CHUNKS + c) * part * 4
            for q in range(4):
                rows = pieces[c][s, 0, q].astype(jnp.float32)
                for j in range(scratch.shape[0]):
                    block = rows[:, j * 128 : (j + 1) * 128]
                    scratch[j, pl.ds(first + q, part, stride=4), :] = block
    for j in range(scratch.shape[0]):
        out_ref[0, :, j * 128 : (j + 1) * 128] = scratch[j].astype(jnp.bfloat16)


def assemble_call(n, pieces, tokens):
    _, frames, _, part, width = pieces[0].shape
    return pl.pallas_call(
        lambda *refs: assemble_kernel(n, part, *refs),
        grid=(frames,),
        in_specs=[pl.BlockSpec((n, 1, 4, part, width), lambda f: (0, f, 0, 0, 0))] * len(pieces),
        out_specs=pl.BlockSpec((1, tokens, width), lambda f: (f, 0, 0)),
        out_shape=jax.ShapeDtypeStruct((frames, tokens, width), jnp.bfloat16),
        scratch_shapes=[pltpu.VMEM((width // 128, tokens, 128), jnp.float32)],
        name="assemble",
    )(*pieces)


def body(
    video,
    timestep,
    cond_weight,
    spatial_gain,
    spatial_qkv,
    spatial_out,
    temporal_gain,
    temporal_qkv,
    temporal_out,
    merge_weight,
    coarse_gain,
    coarse_qkv,
    coarse_out,
    up_weight,
):
    frames, tokens, width = video.shape
    n = lax.axis_size("frame")
    modulation = modulation_of(timestep, cond_weight)
    scale_s, shift_s, scale_t, shift_t = [
        modulation[i * width : (i + 1) * width].reshape(1, width) for i in range(4)
    ]
    gain_s = spatial_gain.reshape(1, width) * (1.0 + scale_s)
    gain_t = temporal_gain.reshape(1, width) * (1.0 + scale_t)

    def exchange(array):
        return lax.all_to_all(array, "frame", 0, 0, tiled=True)

    landed = [
        [exchange(a) for a in spatial_call(n, f, video, gain_s, shift_s, spatial_qkv, spatial_out)]
        for f in range(frames)
    ]
    vectors = (gain_t, shift_t, coarse_gain.reshape(1, -1))
    weights = (temporal_qkv, temporal_out, merge_weight, coarse_qkv, coarse_out, up_weight)
    home = [
        exchange(window_call(n, frames, [pair[c] for pair in landed], vectors, weights))
        for c in range(CHUNKS)
    ]
    return assemble_call(n, home, tokens)


def solution(mesh):
    n = mesh.shape["frame"]
    whole = P(("clip", "frame"), None, None)

    def chosen(video, *rest):
        tiled = video.shape[1] % (4 * n * CHUNKS * 8) == 0 and video.shape[0] % 2 == 0
        return (body if tiled else body_small)(video, *rest)

    return jax.shard_map(
        chosen,
        mesh=mesh,
        in_specs=(whole, P("clip")) + (P(),) * 12,
        out_specs=whole,
        check_vma=False,
    )
```

```python
import math

import jax
import jax.numpy as jnp
from jax import lax
from jax.experimental import pallas as pl
from jax.experimental.pallas import tpu as pltpu
from jax.sharding import PartitionSpec as P

D = 512
DC = 1024
HEAD = 64
FREQ = 64


def modulation_of(timestep, cond_weight):
    counter = jnp.arange(FREQ, dtype=jnp.float32)
    frequency = jnp.exp(counter * (-math.log(10000.0) / FREQ))
    angles = timestep.astype(jnp.float32)[0] * frequency
    embedding = jnp.concatenate([jnp.sin(angles), jnp.cos(angles)])
    return jnp.dot(
        embedding[None, :], cond_weight.astype(jnp.float32), precision=lax.Precision.HIGHEST
    )[0]


def attention_block(inputs, gain_vec, scale_mod, shift_mod, w_qkv, w_out, head_count):
    length, batched, features = inputs.shape
    widened = inputs.astype(jnp.float32)
    mean_square = jnp.mean(widened * widened, axis=-1, keepdims=True)
    normed = (
        widened * lax.rsqrt(mean_square + 1e-06) * gain_vec * (1.0 + scale_mod) + shift_mod
    ).astype(jnp.bfloat16)
    projected = jnp.dot(
        normed.reshape(length * batched, features), w_qkv, preferred_element_type=jnp.float32
    )
    projected = projected.astype(jnp.bfloat16).reshape(
        length, batched, 3, head_count, features // head_count
    )
    queries = projected[:, :, 0]
    keys = projected[:, :, 1]
    values = projected[:, :, 2]
    scores = jnp.einsum("snhe,tnhe->nhst", queries, keys, preferred_element_type=jnp.float32) * (
        1.0 / math.sqrt(features // head_count)
    )
    probs = jax.nn.softmax(scores, axis=-1).astype(jnp.bfloat16)
    mixed = jnp.einsum("nhst,tnhe->snhe", probs, values, preferred_element_type=jnp.float32)
    mixed = mixed.astype(jnp.bfloat16).reshape(length * batched, features)
    update = jnp.dot(mixed, w_out, preferred_element_type=jnp.float32).reshape(
        length, batched, features
    )
    return (widened + update).astype(jnp.bfloat16)


def merge_frames(fine_tokens, merge_weight):
    frames_here, blocks, quads, features = fine_tokens.shape
    paired = fine_tokens.reshape(frames_here // 2, 2, blocks, quads, features).transpose(
        0, 2, 1, 3, 4
    )
    paired = paired.reshape(frames_here // 2 * blocks, 2 * quads * features)
    merged = jnp.dot(paired, merge_weight, preferred_element_type=jnp.float32).astype(jnp.bfloat16)
    return merged.reshape(frames_here // 2, blocks, merge_weight.shape[1])


def combine_levels(fine_tokens, coarse_tokens, up_weight):
    frames_here, blocks, quads, features = fine_tokens.shape
    upsampled = jnp.dot(
        coarse_tokens.reshape(-1, coarse_tokens.shape[2]),
        up_weight,
        preferred_element_type=jnp.float32,
    )
    upsampled = upsampled.reshape(frames_here // 2, 1, blocks, 1, features)
    result = (
        fine_tokens.astype(jnp.float32).reshape(frames_here // 2, 2, blocks, quads, features)
        + upsampled
    )
    return result.astype(jnp.bfloat16).reshape(fine_tokens.shape)


def body_small(
    video,
    timestep,
    cond_weight,
    spatial_gain,
    spatial_qkv,
    spatial_out,
    temporal_gain,
    temporal_qkv,
    temporal_out,
    merge_weight,
    coarse_gain,
    coarse_qkv,
    coarse_out,
    up_weight,
):
    frames_local, tokens_frame, features = video.shape
    groups = lax.axis_size("frame")
    cells_local = tokens_frame // 4 // groups
    modulation = modulation_of(timestep, cond_weight)
    scale_s, shift_s, scale_t, shift_t = [modulation[i * D : (i + 1) * D] for i in range(4)]

    def spatial(frame_rows):
        return attention_block(
            frame_rows[:, None, :],
            spatial_gain,
            scale_s,
            shift_s,
            spatial_qkv,
            spatial_out,
            D // HEAD,
        )[:, 0, :]

    fine1 = lax.map(spatial, video)
    grouped = fine1.reshape(frames_local, groups, cells_local, 4, features)
    cell_view = lax.all_to_all(grouped, "frame", split_axis=1, concat_axis=0, tiled=True)
    length = cell_view.shape[0]
    single = cell_view.shape[1]
    blocks = cell_view.shape[2]
    cell_rows = cell_view.reshape(length, single * blocks, 4, features)
    temporal_length = cell_rows.shape[0]
    temporal_blocks = cell_rows.shape[1]
    mixed = attention_block(
        cell_rows.reshape(temporal_length, temporal_blocks * 4, features),
        temporal_gain,
        scale_t,
        shift_t,
        temporal_qkv,
        temporal_out,
        D // HEAD,
    )
    fine2 = mixed.reshape(cell_rows.shape)
    coarse0 = merge_frames(fine2, merge_weight)
    coarse1 = attention_block(coarse0, coarse_gain, 0.0, 0.0, coarse_qkv, coarse_out, DC // HEAD)
    exchanged = combine_levels(fine2, coarse1, up_weight).reshape(cell_view.shape)
    result = lax.all_to_all(exchanged, "frame", split_axis=0, concat_axis=1, tiled=True)
    return result.reshape(frames_local, tokens_frame, features)


CHUNKS = 2
LOG2E = math.log2(math.e)
ANY = pl.BlockSpec(memory_space=pl.ANY)
VMEM = pl.BlockSpec(memory_space=pltpu.VMEM)


def dot(a, b):
    return jnp.dot(a, b, preferred_element_type=jnp.float32)


def dot_t(a, b):
    return lax.dot_general(a, b, (((1,), (1,)), ((), ())), preferred_element_type=jnp.float32)


def normed_rows(x, gain, shift):
    mean_square = jnp.mean(x * x, axis=-1, keepdims=True)
    y = x * lax.rsqrt(mean_square + 1e-06) * gain
    return (y if shift is None else y + shift).astype(jnp.bfloat16)


def project(normed, w_ref, qkv_ref, width, step=512):
    for i in range(0, 3 * width, step):
        part = dot(normed, w_ref[:, i : i + step])
        if i < width:
            part = part * (LOG2E / math.sqrt(HEAD))
        qkv_ref[:, i : i + step] = part.astype(jnp.bfloat16)


def attend(qkv_ref, mixed_ref, width, bias, block):
    rows = qkv_ref.shape[0]
    low = lax.broadcasted_iota(jnp.int32, (1, 2 * HEAD), 1) < HEAD
    for pair in range(width // (2 * HEAD)):
        at = pair * 2 * HEAD
        keys = qkv_ref[:, width + at : width + at + 2 * HEAD]
        values = qkv_ref[:, 2 * width + at : 2 * width + at + 2 * HEAD]
        zero = jnp.zeros_like(keys)
        one = jnp.ones_like(keys)
        sides = (
            (jnp.where(low, keys, zero), jnp.where(low, values, one)),
            (jnp.where(low, zero, keys), jnp.where(low, one, values)),
        )
        for r in range(0, rows, block):
            queries = qkv_ref[r : r + block, at : at + 2 * HEAD]
            got = []
            for k_side, v_side in sides:
                scores = dot_t(queries, k_side)
                if bias is not None:
                    scores = scores + bias
                probs = jnp.exp2(scores - jnp.max(scores, axis=-1, keepdims=True))
                got.append(dot(probs.astype(jnp.bfloat16), v_side))
            top = jnp.where(low, got[0], got[1])
            sums = pltpu.roll(jnp.where(low, got[1], got[0]), HEAD, 1)
            mixed_ref[r : r + block, at : at + 2 * HEAD] = (top / sums).astype(jnp.bfloat16)


def spatial_kernel(
    n, x_ref, gain_ref, shift_ref, w_ref, wo_ref, *rest
):
    outs, (xs, xp, qkv, mixed) = rest[:-4], rest[-4:]
    tokens, width = mixed.shape
    cells = tokens // 4
    part = cells // n // CHUNKS
    for j in range(width // 128):
        xs[j] = x_ref[0, :, j * 128 : (j + 1) * 128].astype(jnp.float32)
        for q in range(4):
            xp[q, :, j * 128 : (j + 1) * 128] = xs[j, pl.ds(q, cells, stride=4), :]
    x = xp[...].reshape(tokens, width)
    project(normed_rows(x, gain_ref[...], shift_ref[...]), w_ref, qkv, width)
    attend(qkv, mixed, width, None, 256)
    done = xp[...].reshape(tokens, width) + dot(mixed[...], wo_ref[...])
    xp[...] = done.reshape(xp.shape)
    for s in range(n):
        for c in range(CHUNKS):
            first = (s * CHUNKS + c) * part
            piece = xp[:, first : first + part, :].astype(jnp.bfloat16)
            if len(outs) == 1:
                outs[0][s, 0, c] = piece
            else:
                outs[c][s, 0] = piece


def spatial_call(n, first, count, together, video, gain, shift, w, wo):
    _, tokens, width = video.shape
    part = tokens // 4 // n // CHUNKS
    tail = (4, part, width)
    if together:
        out_shape = [jax.ShapeDtypeStruct((n, count, CHUNKS) + tail, jnp.bfloat16)]
        out_specs = [pl.BlockSpec((n, 1, CHUNKS) + tail, lambda i: (0, i, 0, 0, 0, 0))]
    else:
        out_shape = [jax.ShapeDtypeStruct((n, count) + tail, jnp.bfloat16)] * CHUNKS
        out_specs = [pl.BlockSpec((n, 1) + tail, lambda i: (0, i, 0, 0, 0))] * CHUNKS
    return pl.pallas_call(
        lambda *refs: spatial_kernel(n, *refs),
        grid=(count,),
        in_specs=[
            pl.BlockSpec((1, tokens, width), lambda i: (first + i, 0, 0)),
            VMEM,
            VMEM,
            VMEM,
            VMEM,
        ],
        out_specs=out_specs,
        out_shape=out_shape,
        scratch_shapes=[
            pltpu.VMEM((width // 128, tokens, 128), jnp.float32),
            pltpu.VMEM((4, tokens // 4, width), jnp.float32),
            pltpu.VMEM((tokens, 3 * width), jnp.bfloat16),
            pltpu.VMEM((tokens, width), jnp.bfloat16),
        ],
        cost_estimate=pl.CostEstimate(
            flops=count * (8 * tokens * width * width + 8 * tokens * tokens * width),
            bytes_accessed=8 * width * width + count * 4 * tokens * width,
            transcendentals=count * tokens * tokens * width // HEAD,
        ),
        name="spatial",
    )(video, gain, shift, w, wo)


def same_cell(rows, part):
    a = lax.rem(lax.broadcasted_iota(jnp.int32, (rows, rows), 0), part)
    b = lax.rem(lax.broadcasted_iota(jnp.int32, (rows, rows), 1), part)
    return jnp.where(a == b, 0.0, -1e30).astype(jnp.float32)


def window_kernel(n, frames, part, groups, *refs):
    pieces, refs = refs[:groups], refs[groups:]
    gain, shift, coarse_gain, *hbm, out_ref = refs[:10]
    xs, qkv, mixed, bias, cqkv, cmixed, *held, sems = refs[10:]
    copies = [pltpu.make_async_copy(hbm[i], held[i], sems.at[i]) for i in range(6)]
    for copy in copies:
        copy.start()
    wt, wto, wm, wc, wco, wu = held
    rows, width = mixed.shape
    coarse_rows, coarse_width = cmixed.shape
    bias[...] = same_cell(rows, part)
    for s in range(n):
        for f in range(frames):
            at = (s * frames + f) * part
            g, i = divmod(f, frames // groups)
            piece = pieces[g]
            for q in range(4):
                rows_q = piece[s, i, 0, q] if len(piece.shape) == 6 else piece[s, i, q]
                xs[q, at : at + part, :] = rows_q.astype(jnp.float32)
    copies[0].wait()
    copies[1].wait()

    def temporal(q, carry):
        project(normed_rows(xs[q], gain[...], shift[...]), wt, qkv, width)
        attend(qkv, mixed, width, bias[...], rows)
        fine = xs[q] + dot(mixed[...], wto[...])
        xs[q] = fine.astype(jnp.bfloat16).astype(jnp.float32)
        return carry

    lax.fori_loop(0, 4, temporal, 0)
    copies[2].wait()
    coarse = None
    for d in range(2):
        for q in range(4):
            fine = xs[q].reshape(coarse_rows // part, 2, part, width)[:, d]
            fine = fine.reshape(coarse_rows, width).astype(jnp.bfloat16)
            at = (d * 4 + q) * width
            term = dot(fine, wm[at : at + width, :])
            coarse = term if coarse is None else coarse + term
    coarse = coarse.astype(jnp.bfloat16).astype(jnp.float32)
    copies[3].wait()
    project(normed_rows(coarse, coarse_gain[...], None), wc, cqkv, coarse_width)
    attend(cqkv, cmixed, coarse_width, bias[:coarse_rows, :coarse_rows], coarse_rows)
    copies[4].wait()
    coarse = (coarse + dot(cmixed[...], wco[...])).astype(jnp.bfloat16)
    copies[5].wait()
    up = dot(coarse, wu[...])
    for s in range(n):
        for f in range(frames):
            at = (s * frames + f) * part
            pair = at // (2 * part) * part
            for q in range(4):
                done = xs[q, at : at + part, :] + up[pair : pair + part]
                out_ref[s, f, q] = done.astype(jnp.bfloat16)


def window_call(n, frames, chunk, pieces, vectors, weights):
    part, width = pieces[0].shape[-2:]

    def spec(a):
        if a.ndim == 5:
            return VMEM
        shape = a.shape[:2] + (1,) + a.shape[3:]
        return pl.BlockSpec(shape, lambda i: (0, 0, chunk, 0, 0, 0))

    rows = n * frames * part
    coarse_width = weights[3].shape[0]
    flops = 2 * 4 * rows * (4 * width * width) + rows * 8 * width * coarse_width
    flops += rows * (4 * coarse_width * coarse_width + coarse_width * width)
    return pl.pallas_call(
        lambda *refs: window_kernel(n, frames, part, len(pieces), *refs),
        grid=(1,),
        in_specs=[spec(a) for a in pieces] + [VMEM] * 3 + [ANY] * 6,
        out_specs=VMEM,
        out_shape=jax.ShapeDtypeStruct((n, frames, 4, part, width), jnp.bfloat16),
        scratch_shapes=[
            pltpu.VMEM((4, rows, width), jnp.float32),
            pltpu.VMEM((rows, 3 * width), jnp.bfloat16),
            pltpu.VMEM((rows, width), jnp.bfloat16),
            pltpu.VMEM((rows, rows), jnp.float32),
            pltpu.VMEM((rows // 2, 3 * coarse_width), jnp.bfloat16),
            pltpu.VMEM((rows // 2, coarse_width), jnp.bfloat16),
        ]
        + [pltpu.VMEM(w.shape, w.dtype) for w in weights]
        + [pltpu.SemaphoreType.DMA((6,))],
        cost_estimate=pl.CostEstimate(
            flops=flops,
            bytes_accessed=sum(w.size for w in weights) * 2 + 16 * rows * width,
            transcendentals=4 * rows * rows * width // HEAD,
        ),
        name="window",
    )(*pieces, *vectors, *weights)


def assemble_kernel(n, part, *refs):
    pieces, out_ref, scratch = refs[:-2], refs[-2], refs[-1]
    for s in range(n):
        for c in range(CHUNKS):
            first = (s * CHUNKS + c) * part * 4
            for q in range(4):
                rows = pieces[c][s, 0, q].astype(jnp.float32)
                for j in range(scratch.shape[0]):
                    block = rows[:, j * 128 : (j + 1) * 128]
                    scratch[j, pl.ds(first + q, part, stride=4), :] = block
    for j in range(scratch.shape[0]):
        out_ref[0, :, j * 128 : (j + 1) * 128] = scratch[j].astype(jnp.bfloat16)


def assemble_call(n, pieces, tokens):
    _, frames, _, part, width = pieces[0].shape
    return pl.pallas_call(
        lambda *refs: assemble_kernel(n, part, *refs),
        grid=(frames,),
        in_specs=[pl.BlockSpec((n, 1, 4, part, width), lambda f: (0, f, 0, 0, 0))] * len(pieces),
        out_specs=pl.BlockSpec((1, tokens, width), lambda f: (f, 0, 0)),
        out_shape=jax.ShapeDtypeStruct((frames, tokens, width), jnp.bfloat16),
        scratch_shapes=[pltpu.VMEM((width // 128, tokens, 128), jnp.float32)],
        name="assemble",
    )(*pieces)


def body(
    video,
    timestep,
    cond_weight,
    spatial_gain,
    spatial_qkv,
    spatial_out,
    temporal_gain,
    temporal_qkv,
    temporal_out,
    merge_weight,
    coarse_gain,
    coarse_qkv,
    coarse_out,
    up_weight,
):
    frames, tokens, width = video.shape
    n = lax.axis_size("frame")
    modulation = modulation_of(timestep, cond_weight)
    scale_s, shift_s, scale_t, shift_t = [
        modulation[i * width : (i + 1) * width].reshape(1, width) for i in range(4)
    ]
    gain_s = spatial_gain.reshape(1, width) * (1.0 + scale_s)
    gain_t = temporal_gain.reshape(1, width) * (1.0 + scale_t)

    def exchange(array):
        return lax.all_to_all(array, "frame", 0, 0, tiled=True)

    block = (video, gain_s, shift_s, spatial_qkv, spatial_out)
    half = frames // 2
    early = [exchange(a) for a in spatial_call(n, 0, half, True, *block)]
    late = [exchange(a) for a in spatial_call(n, half, frames - half, False, *block)]
    vectors = (gain_t, shift_t, coarse_gain.reshape(1, -1))
    weights = (temporal_qkv, temporal_out, merge_weight, coarse_qkv, coarse_out, up_weight)
    home = [
        exchange(window_call(n, frames, c, [early[0], late[c]], vectors, weights))
        for c in range(CHUNKS)
    ]
    return assemble_call(n, home, tokens)


def solution(mesh):
    n = mesh.shape["frame"]
    whole = P(("clip", "frame"), None, None)

    def chosen(video, *rest):
        tiled = video.shape[1] % (4 * n * CHUNKS * 8) == 0 and video.shape[0] % 2 == 0
        return (body if tiled else body_small)(video, *rest)

    return jax.shard_map(
        chosen,
        mesh=mesh,
        in_specs=(whole, P("clip")) + (P(),) * 12,
        out_specs=whole,
        check_vma=False,
    )
```

```python
import math

import jax
import jax.numpy as jnp
from jax import lax
from jax.experimental import pallas as pl
from jax.experimental.pallas import tpu as pltpu
from jax.sharding import PartitionSpec as P

D = 512
DC = 1024
HEAD = 64
FREQ = 64


def modulation_of(timestep, cond_weight):
    counter = jnp.arange(FREQ, dtype=jnp.float32)
    frequency = jnp.exp(counter * (-math.log(10000.0) / FREQ))
    angles = timestep.astype(jnp.float32)[0] * frequency
    embedding = jnp.concatenate([jnp.sin(angles), jnp.cos(angles)])
    return jnp.dot(
        embedding[None, :], cond_weight.astype(jnp.float32), precision=lax.Precision.HIGHEST
    )[0]


def attention_block(inputs, gain_vec, scale_mod, shift_mod, w_qkv, w_out, head_count):
    length, batched, features = inputs.shape
    widened = inputs.astype(jnp.float32)
    mean_square = jnp.mean(widened * widened, axis=-1, keepdims=True)
    normed = (
        widened * lax.rsqrt(mean_square + 1e-06) * gain_vec * (1.0 + scale_mod) + shift_mod
    ).astype(jnp.bfloat16)
    projected = jnp.dot(
        normed.reshape(length * batched, features), w_qkv, preferred_element_type=jnp.float32
    )
    projected = projected.astype(jnp.bfloat16).reshape(
        length, batched, 3, head_count, features // head_count
    )
    queries = projected[:, :, 0]
    keys = projected[:, :, 1]
    values = projected[:, :, 2]
    scores = jnp.einsum("snhe,tnhe->nhst", queries, keys, preferred_element_type=jnp.float32) * (
        1.0 / math.sqrt(features // head_count)
    )
    probs = jax.nn.softmax(scores, axis=-1).astype(jnp.bfloat16)
    mixed = jnp.einsum("nhst,tnhe->snhe", probs, values, preferred_element_type=jnp.float32)
    mixed = mixed.astype(jnp.bfloat16).reshape(length * batched, features)
    update = jnp.dot(mixed, w_out, preferred_element_type=jnp.float32).reshape(
        length, batched, features
    )
    return (widened + update).astype(jnp.bfloat16)


def merge_frames(fine_tokens, merge_weight):
    frames_here, blocks, quads, features = fine_tokens.shape
    paired = fine_tokens.reshape(frames_here // 2, 2, blocks, quads, features).transpose(
        0, 2, 1, 3, 4
    )
    paired = paired.reshape(frames_here // 2 * blocks, 2 * quads * features)
    merged = jnp.dot(paired, merge_weight, preferred_element_type=jnp.float32).astype(jnp.bfloat16)
    return merged.reshape(frames_here // 2, blocks, merge_weight.shape[1])


def combine_levels(fine_tokens, coarse_tokens, up_weight):
    frames_here, blocks, quads, features = fine_tokens.shape
    upsampled = jnp.dot(
        coarse_tokens.reshape(-1, coarse_tokens.shape[2]),
        up_weight,
        preferred_element_type=jnp.float32,
    )
    upsampled = upsampled.reshape(frames_here // 2, 1, blocks, 1, features)
    result = (
        fine_tokens.astype(jnp.float32).reshape(frames_here // 2, 2, blocks, quads, features)
        + upsampled
    )
    return result.astype(jnp.bfloat16).reshape(fine_tokens.shape)


def body_small(
    video,
    timestep,
    cond_weight,
    spatial_gain,
    spatial_qkv,
    spatial_out,
    temporal_gain,
    temporal_qkv,
    temporal_out,
    merge_weight,
    coarse_gain,
    coarse_qkv,
    coarse_out,
    up_weight,
):
    frames_local, tokens_frame, features = video.shape
    groups = lax.axis_size("frame")
    cells_local = tokens_frame // 4 // groups
    modulation = modulation_of(timestep, cond_weight)
    scale_s, shift_s, scale_t, shift_t = [modulation[i * D : (i + 1) * D] for i in range(4)]

    def spatial(frame_rows):
        return attention_block(
            frame_rows[:, None, :],
            spatial_gain,
            scale_s,
            shift_s,
            spatial_qkv,
            spatial_out,
            D // HEAD,
        )[:, 0, :]

    fine1 = lax.map(spatial, video)
    grouped = fine1.reshape(frames_local, groups, cells_local, 4, features)
    cell_view = lax.all_to_all(grouped, "frame", split_axis=1, concat_axis=0, tiled=True)
    length = cell_view.shape[0]
    single = cell_view.shape[1]
    blocks = cell_view.shape[2]
    cell_rows = cell_view.reshape(length, single * blocks, 4, features)
    temporal_length = cell_rows.shape[0]
    temporal_blocks = cell_rows.shape[1]
    mixed = attention_block(
        cell_rows.reshape(temporal_length, temporal_blocks * 4, features),
        temporal_gain,
        scale_t,
        shift_t,
        temporal_qkv,
        temporal_out,
        D // HEAD,
    )
    fine2 = mixed.reshape(cell_rows.shape)
    coarse0 = merge_frames(fine2, merge_weight)
    coarse1 = attention_block(coarse0, coarse_gain, 0.0, 0.0, coarse_qkv, coarse_out, DC // HEAD)
    exchanged = combine_levels(fine2, coarse1, up_weight).reshape(cell_view.shape)
    result = lax.all_to_all(exchanged, "frame", split_axis=0, concat_axis=1, tiled=True)
    return result.reshape(frames_local, tokens_frame, features)


CHUNKS = 2
LOG2E = math.log2(math.e)
ANY = pl.BlockSpec(memory_space=pl.ANY)
VMEM = pl.BlockSpec(memory_space=pltpu.VMEM)


def dot(a, b):
    return jnp.dot(a, b, preferred_element_type=jnp.float32)


def dot_t(a, b):
    return lax.dot_general(a, b, (((1,), (1,)), ((), ())), preferred_element_type=jnp.float32)


def normed_rows(x, gain, shift):
    mean_square = jnp.mean(x * x, axis=-1, keepdims=True)
    y = x * lax.rsqrt(mean_square + 1e-06) * gain
    return (y if shift is None else y + shift).astype(jnp.bfloat16)


def project(normed, w_ref, qkv_ref, width, step=512):
    for i in range(0, 3 * width, step):
        part = dot(normed, w_ref[:, i : i + step])
        if i < width:
            part = part * (LOG2E / math.sqrt(HEAD))
        qkv_ref[:, i : i + step] = part.astype(jnp.bfloat16)


def attend(qkv_ref, mixed_ref, width, bias, block):
    rows = qkv_ref.shape[0]
    low = lax.broadcasted_iota(jnp.int32, (1, 2 * HEAD), 1) < HEAD
    for pair in range(width // (2 * HEAD)):
        at = pair * 2 * HEAD
        keys = qkv_ref[:, width + at : width + at + 2 * HEAD]
        values = qkv_ref[:, 2 * width + at : 2 * width + at + 2 * HEAD]
        zero = jnp.zeros_like(keys)
        one = jnp.ones_like(keys)
        sides = (
            (jnp.where(low, keys, zero), jnp.where(low, values, one)),
            (jnp.where(low, zero, keys), jnp.where(low, one, values)),
        )
        for r in range(0, rows, block):
            queries = qkv_ref[r : r + block, at : at + 2 * HEAD]
            got = []
            for k_side, v_side in sides:
                scores = dot_t(queries, k_side)
                if bias is not None:
                    scores = scores + bias
                probs = jnp.exp2(scores - jnp.max(scores, axis=-1, keepdims=True))
                got.append(dot(probs.astype(jnp.bfloat16), v_side))
            top = jnp.where(low, got[0], got[1])
            sums = pltpu.roll(jnp.where(low, got[1], got[0]), HEAD, 1)
            mixed_ref[r : r + block, at : at + 2 * HEAD] = (top / sums).astype(jnp.bfloat16)


def spatial_kernel(n, x_ref, gain_ref, shift_ref, w_ref, wo_ref, *rest):
    outs, (xs, xp, qkv, mixed) = rest[-4 - CHUNKS : -4], rest[-4:]
    tokens, width = mixed.shape
    cells = tokens // 4
    part = cells // n // CHUNKS
    for j in range(width // 128):
        xs[j] = x_ref[0, :, j * 128 : (j + 1) * 128].astype(jnp.float32)
        for q in range(4):
            xp[q, :, j * 128 : (j + 1) * 128] = xs[j, pl.ds(q, cells, stride=4), :]
    x = xp[...].reshape(tokens, width)
    project(normed_rows(x, gain_ref[...], shift_ref[...]), w_ref, qkv, width)
    attend(qkv, mixed, width, None, 256)
    done = xp[...].reshape(tokens, width) + dot(mixed[...], wo_ref[...])
    xp[...] = done.reshape(xp.shape)
    for s in range(n):
        for c in range(CHUNKS):
            first = (s * CHUNKS + c) * part
            outs[c][s, 0] = xp[:, first : first + part, :].astype(jnp.bfloat16)


def spatial_call(n, first, count, rest, video, gain, shift, w, wo):
    frames, tokens, width = video.shape
    tail = (4, tokens // 4 // n // CHUNKS, width)
    taken = [] if rest is None else [rest]
    return pl.pallas_call(
        lambda *refs: spatial_kernel(n, *refs),
        grid=(count,),
        in_specs=[
            pl.BlockSpec((1, tokens, width), lambda i: (first + i, 0, 0)),
            VMEM,
            VMEM,
            VMEM,
            VMEM,
        ]
        + [ANY] * len(taken),
        out_specs=[
            pl.BlockSpec((n, 1) + tail, lambda i: (0, i, 0, 0, 0)),
            pl.BlockSpec((n, 1) + tail, lambda i: (0, first + i, 0, 0, 0)),
        ],
        out_shape=[
            jax.ShapeDtypeStruct((n, count) + tail, jnp.bfloat16),
            jax.ShapeDtypeStruct((n, frames) + tail, jnp.bfloat16),
        ],
        input_output_aliases={5: 1} if taken else {},
        scratch_shapes=[
            pltpu.VMEM((width // 128, tokens, 128), jnp.float32),
            pltpu.VMEM((4, tokens // 4, width), jnp.float32),
            pltpu.VMEM((tokens, 3 * width), jnp.bfloat16),
            pltpu.VMEM((tokens, width), jnp.bfloat16),
        ],
        cost_estimate=pl.CostEstimate(
            flops=count * (8 * tokens * width * width + 8 * tokens * tokens * width),
            bytes_accessed=8 * width * width + count * 4 * tokens * width,
            transcendentals=count * tokens * tokens * width // HEAD,
        ),
        name="spatial",
    )(video, gain, shift, w, wo, *taken)


def same_cell(rows, part):
    a = lax.rem(lax.broadcasted_iota(jnp.int32, (rows, rows), 0), part)
    b = lax.rem(lax.broadcasted_iota(jnp.int32, (rows, rows), 1), part)
    return jnp.where(a == b, 0.0, -1e30).astype(jnp.float32)


def window_kernel(n, frames, part, groups, *refs):
    pieces, refs = refs[:groups], refs[groups:]
    gain, shift, coarse_gain, *hbm, out_ref = refs[:10]
    xs, qkv, mixed, bias, cqkv, cmixed, ordered, *held, sems = refs[10:]
    copies = [pltpu.make_async_copy(hbm[i], held[i], sems.at[i]) for i in range(6)]
    for copy in copies:
        copy.start()
    wt, wto, wm, wc, wco, wu = held
    rows, width = mixed.shape
    coarse_rows, coarse_width = cmixed.shape
    bias[...] = same_cell(rows, part)
    for s in range(n):
        for f in range(frames):
            at = (s * frames + f) * part
            g, i = divmod(f, frames // groups)
            for q in range(4):
                xs[q, at : at + part, :] = pieces[g][s, i, q].astype(jnp.float32)
    copies[0].wait()
    copies[1].wait()

    def temporal(q, carry):
        project(normed_rows(xs[q], gain[...], shift[...]), wt, qkv, width)
        attend(qkv, mixed, width, bias[...], rows)
        fine = xs[q] + dot(mixed[...], wto[...])
        xs[q] = fine.astype(jnp.bfloat16).astype(jnp.float32)
        return carry

    lax.fori_loop(0, 4, temporal, 0)
    copies[2].wait()
    coarse = None
    for d in range(2):
        for q in range(4):
            fine = xs[q].reshape(coarse_rows // part, 2, part, width)[:, d]
            fine = fine.reshape(coarse_rows, width).astype(jnp.bfloat16)
            at = (d * 4 + q) * width
            term = dot(fine, wm[at : at + width, :])
            coarse = term if coarse is None else coarse + term
    coarse = coarse.astype(jnp.bfloat16).astype(jnp.float32)
    copies[3].wait()
    project(normed_rows(coarse, coarse_gain[...], None), wc, cqkv, coarse_width)
    attend(cqkv, cmixed, coarse_width, bias[:coarse_rows, :coarse_rows], coarse_rows)
    copies[4].wait()
    coarse = (coarse + dot(cmixed[...], wco[...])).astype(jnp.bfloat16)
    copies[5].wait()
    up = dot(coarse, wu[...])
    for s in range(n):
        for f in range(frames):
            at = (s * frames + f) * part
            pair = at // (2 * part) * part
            for q in range(4):
                done = xs[q, at : at + part, :] + up[pair : pair + part]
                for j in range(width // 128):
                    lanes = done[:, j * 128 : (j + 1) * 128]
                    ordered[j, pl.ds(4 * at + q, part, stride=4), :] = lanes
    for s in range(n):
        for f in range(frames):
            at = (s * frames + f) * part * 4
            for j in range(width // 128):
                lanes = ordered[j, at : at + 4 * part, :]
                out_ref[s, f, :, j * 128 : (j + 1) * 128] = lanes.astype(jnp.bfloat16)


def window_call(n, frames, pieces, vectors, weights):
    part, width = pieces[0].shape[-2:]
    rows = n * frames * part
    coarse_width = weights[3].shape[0]
    flops = 2 * 4 * rows * (4 * width * width) + rows * 8 * width * coarse_width
    flops += rows * (4 * coarse_width * coarse_width + coarse_width * width)
    return pl.pallas_call(
        lambda *refs: window_kernel(n, frames, part, len(pieces), *refs),
        in_specs=[VMEM] * (len(pieces) + 3) + [ANY] * 6,
        out_specs=VMEM,
        out_shape=jax.ShapeDtypeStruct((n, frames, 4 * part, width), jnp.bfloat16),
        scratch_shapes=[
            pltpu.VMEM((4, rows, width), jnp.float32),
            pltpu.VMEM((rows, 3 * width), jnp.bfloat16),
            pltpu.VMEM((rows, width), jnp.bfloat16),
            pltpu.VMEM((rows, rows), jnp.float32),
            pltpu.VMEM((rows // 2, 3 * coarse_width), jnp.bfloat16),
            pltpu.VMEM((rows // 2, coarse_width), jnp.bfloat16),
            pltpu.VMEM((width // 128, 4 * rows, 128), jnp.float32),
        ]
        + [pltpu.VMEM(w.shape, w.dtype) for w in weights]
        + [pltpu.SemaphoreType.DMA((6,))],
        cost_estimate=pl.CostEstimate(
            flops=flops,
            bytes_accessed=sum(w.size for w in weights) * 2 + 16 * rows * width,
            transcendentals=4 * rows * rows * width // HEAD,
        ),
        name="window",
    )(*pieces, *vectors, *weights)


def place_kernel(piece_ref, *refs):
    refs[-1][0, :, 0] = piece_ref[:, 0]


def place_call(chunk, piece, result):
    n, frames, rows, width = piece.shape
    taken = [] if result is None else [result]
    return pl.pallas_call(
        place_kernel,
        grid=(frames,),
        in_specs=[pl.BlockSpec((n, 1, rows, width), lambda f: (0, f, 0, 0))] + [ANY] * len(taken),
        out_specs=pl.BlockSpec((1, n, 1, rows, width), lambda f: (f, 0, chunk, 0, 0)),
        out_shape=jax.ShapeDtypeStruct((frames, n, CHUNKS, rows, width), jnp.bfloat16),
        input_output_aliases={1: 0} if taken else {},
        cost_estimate=pl.CostEstimate(
            flops=0, bytes_accessed=4 * piece.size, transcendentals=0
        ),
        name="place",
    )(piece, *taken)


def body(
    video,
    timestep,
    cond_weight,
    spatial_gain,
    spatial_qkv,
    spatial_out,
    temporal_gain,
    temporal_qkv,
    temporal_out,
    merge_weight,
    coarse_gain,
    coarse_qkv,
    coarse_out,
    up_weight,
):
    frames, tokens, width = video.shape
    n = lax.axis_size("frame")
    modulation = modulation_of(timestep, cond_weight)
    scale_s, shift_s, scale_t, shift_t = [
        modulation[i * width : (i + 1) * width].reshape(1, width) for i in range(4)
    ]
    gain_s = spatial_gain.reshape(1, width) * (1.0 + scale_s)
    gain_t = temporal_gain.reshape(1, width) * (1.0 + scale_t)

    def exchange(array):
        return lax.all_to_all(array, "frame", 0, 0, tiled=True)

    block = (video, gain_s, shift_s, spatial_qkv, spatial_out)
    half = frames // 2
    early, rest = spatial_call(n, 0, half, None, *block)
    early = exchange(early)
    late, rest = spatial_call(n, half, frames - half, rest, *block)
    late = exchange(late)
    rest = exchange(rest)
    vectors = (gain_t, shift_t, coarse_gain.reshape(1, -1))
    weights = (temporal_qkv, temporal_out, merge_weight, coarse_qkv, coarse_out, up_weight)
    home = []
    for pieces in ((early, late), (rest,)):
        part = window_call(n, frames, pieces, vectors, weights)
        home.append(exchange(part))
    result = None
    for c in range(CHUNKS):
        result = place_call(c, home[c], result)
    return result.reshape(frames, tokens, width)


def solution(mesh):
    whole = P(("clip", "frame"), None, None)

    def chosen(video, *rest):
        n = mesh.shape["frame"]
        tiled = video.shape[1] % (4 * n * CHUNKS * 8) == 0 and video.shape[0] % 4 == 0
        return (body if tiled else body_small)(video, *rest)

    return jax.shard_map(
        chosen,
        mesh=mesh,
        in_specs=(whole, P("clip")) + (P(),) * 12,
        out_specs=whole,
        check_vma=False,
    )
```
